1024 devices in a mesh: replica: 8 (over y_hi, core), shard: 128 (over z, x, y_lo).
Axes of the slice: x: 8, y: 8 (y_hi: 4, y_lo: 2; y = y_hi * 2 + y_lo), z: 8, core: 2. Of those that a mesh axis runs over, the one named last changes fastest.
Arguments:
- tokens_in: bfloat16 [131072, 8192], P(('replica', 'shard')), may hold values from -24 to 24
- cotangent: bfloat16 [131072, 128], P(('replica', 'shard')), may hold values from -0.03125 to 0.03125
- next_tokens: bfloat16 [65536, 8192], P(('replica', 'shard')), may hold values from -24 to 24
- master: float32 [8192, 128], P(('replica', 'shard')), may hold values from -0.0625 to 0.0625
- first_moment: float32 [8192, 128], P(('replica', 'shard')), may hold values from -6 to 6
- second_moment: float32 [8192, 128], P(('replica', 'shard')), may hold values from 0.25 to 4
Outputs:
- new_master: float32 [8192, 128], P(('replica', 'shard'))
- new_first: float32 [8192, 128], P(('replica', 'shard'))
- new_second: float32 [8192, 128], P(('replica', 'shard'))
- next_out: bfloat16 [65536, 128], P(('replica', 'shard'))
The draws below stay inside these ranges and needn't reach their ends.
All inputs are finite; a program needn't handle non-finite values.
Results may differ from the reference program's by a relative error of at most 0.005.
Values may be sent and summed in bfloat16 or wider, within the bound.
No kernel may reach another device: no remote copies, remote signals or barrier semaphores. Data moves between devices by JAX's collectives and lax.ppermute only.
A program may use at most 32 MiB of HBM per device.

```python
import math
import jax
import jax.numpy as jnp
from jax import lax

D = 8192
COLS = 128
TOKENS = 131072
NEXT_TOKENS = 65536


def raised(entries, stream_key, source, target, blocks, factor):
    owner, partner = [(jnp.arange(entries.shape[position]) // (entries.shape[position] // blocks)).reshape([-1 if axis == position else 1 for axis in range(entries.ndim)]) for position in (source, target)]
    chosen = jax.random.permutation(stream_key, blocks)[partner]
    strong = (owner == chosen) | (owner == (partner + blocks // 2) % blocks)
    return jnp.where(strong, factor * entries, entries)


def shard_levels(own_key, dims, cuts, least, top_value):
    level = 1.0
    for dim, shards_of in cuts:
        heights = jax.random.uniform(jax.random.fold_in(jax.random.fold_in(own_key, 6), dim), (shards_of,), jnp.float32, least / len(cuts), top_value / len(cuts))
        level = level * jnp.repeat(jnp.exp(heights), dims[dim] // shards_of).reshape((-1,) + (1,) * (len(dims) - 1 - dim))
    return level


def gaussian(key, dims, deviation, reach, pieces=(), kind=jnp.bfloat16):
    entries = jax.random.normal(key, dims, jnp.float32) * deviation
    if len(pieces) > 0:
        entries = shard_levels(key, dims, pieces, -0.22, 0.18) * entries
    return jnp.clip(entries, min=-reach, max=reach).astype(kind)


def gaussian_with(own_key, dims, deviation, reach, pieces, heavy, kind=jnp.bfloat16):
    result = deviation * jax.random.normal(own_key, dims, jnp.float32)
    if pieces:
        result = result * shard_levels(own_key, dims, pieces, -0.22, 0.18)
    return jnp.clip(raised(result, jax.random.fold_in(own_key, 3), *heavy), -reach, reach).astype(kind)


def setup_inputs(seed: int = 0) -> dict:
    keys = jax.random.split(jax.random.key(seed), 7)
    tokens_in = gaussian_with(keys[0], (TOKENS, D), 1.0, 24.0, ((0, 1024),), (0, 1, 1024, 6.0))
    cotangent = gaussian(keys[1], (TOKENS, COLS), (2.0 / (TOKENS ** 0.5)), 0.03125, ((0, 1024),))
    next_tokens = gaussian_with(keys[2], (NEXT_TOKENS, D), 1.0, 24.0, ((0, 1024),), (0, 1, 1024, 6.0))
    master = gaussian(keys[3], (D, COLS), D ** -0.5, 0.0625, ((0, 1024),), jnp.float32)
    first_moment = gaussian(keys[4], (D, COLS), 1.0, 6.0, ((0, 1024),), jnp.float32)
    second_moment = jnp.clip(jnp.exp(math.log(4.0) - 2.7725887 * jax.random.uniform(keys[5], (D, COLS), jnp.float32) ** shard_levels(keys[5], (D, COLS), ((0, 1024),), -0.2, 0.2)), 0.25, 4.0)
    return dict(tokens_in=tokens_in, cotangent=cotangent, next_tokens=next_tokens, master=master, first_moment=first_moment, second_moment=second_moment)


beta_one = 0.9
beta_two = 0.95
learn_rate = 0.003
decay_rate = 0.1
epsilon = 1e-08
steps_done = 10

def reference(tokens_in, cotangent, next_tokens, master, first_moment, second_moment):
    gradient = lax.dot_general(tokens_in, cotangent, (((0,), (0,)), ((), ())), preferred_element_type=jnp.float32)
    new_first = beta_one * first_moment + (1.0 - beta_one) * gradient
    new_second = beta_two * second_moment + (1.0 - beta_two) * gradient * gradient
    first_hat = new_first / (1.0 - beta_one ** steps_done)
    second_hat = new_second / (1.0 - beta_two ** steps_done)
    new_master = master - learn_rate * (first_hat / (jnp.sqrt(second_hat) + epsilon) + decay_rate * master)
    low_weight = new_master.astype(jnp.bfloat16)
    next_out = jnp.dot(next_tokens, low_weight, preferred_element_type=jnp.float32).astype(jnp.bfloat16)
    return (new_master, new_first, new_second, next_out)
```

```python
import jax
import jax.numpy as jnp
from jax import lax
from jax.sharding import Mesh, PartitionSpec as P

beta_one = 0.9
beta_two = 0.95
learn_rate = 0.003
decay_rate = 0.1
epsilon = 1e-08
steps_done = 10

AXES = ("yh", "c", "zh", "zl", "xh", "xl", "yl")
NEAR = ("zl", "xl", "yl")
FAR = ("yh", "zh", "xh")


def on_device(tokens_in, cotangent, next_tokens, master, first_moment, second_moment):
    sizes = [lax.axis_size(a) for a in AXES]
    n_near = lax.axis_size(NEAR)
    n_far = lax.axis_size(FAR)
    model_width = tokens_in.shape[1]
    cols = cotangent.shape[1]
    own_rows = model_width // lax.axis_size(AXES)
    core = lax.axis_index("c")
    swap = [(0, 1), (1, 0)]

    gradient = lax.dot_general(
        tokens_in, cotangent, (((0,), (0,)), ((), ())), preferred_element_type=jnp.float32
    )
    split = gradient.reshape(*sizes, own_rows, cols).transpose(1, 3, 5, 6, 0, 2, 4, 7, 8)
    split = split.reshape(2, n_near, n_far * own_rows, cols)
    keep = lax.dynamic_index_in_dim(split, core, 0, keepdims=False)
    give = lax.dynamic_index_in_dim(split, 1 - core, 0, keepdims=False)
    got = lax.ppermute(give.astype(jnp.bfloat16), "c", swap)
    pair = (keep + got.astype(jnp.float32)).astype(jnp.bfloat16)
    near = lax.all_to_all(pair, NEAR, 0, 0, tiled=True)
    near = jnp.sum(near.astype(jnp.float32), axis=0).astype(jnp.bfloat16)
    far = lax.all_to_all(near.reshape(n_far, own_rows, cols), FAR, 0, 0, tiled=True)
    gradient = jnp.sum(far.astype(jnp.float32), axis=0)

    new_first = beta_one * first_moment + (1.0 - beta_one) * gradient
    new_second = beta_two * second_moment + (1.0 - beta_two) * gradient * gradient
    first_hat = new_first / (1.0 - beta_one**steps_done)
    second_hat = new_second / (1.0 - beta_two**steps_done)
    new_master = master - learn_rate * (
        first_hat / (jnp.sqrt(second_hat) + epsilon) + decay_rate * master
    )
    low_weight = new_master.astype(jnp.bfloat16)

    far = jnp.broadcast_to(low_weight, (n_far, own_rows, cols))
    far = lax.all_to_all(far, FAR, 0, 0, tiled=True).reshape(n_far * own_rows, cols)
    near = jnp.broadcast_to(far, (n_near, n_far * own_rows, cols))
    near = lax.all_to_all(near, NEAR, 0, 0, tiled=True)
    other = lax.ppermute(near, "c", swap)

    by_owner = [sizes[3], sizes[5], sizes[6], sizes[0], sizes[2], sizes[4]]

    def natural(half):
        half = half.reshape(*by_owner, own_rows, cols)
        half = half.transpose(3, 4, 0, 5, 1, 2, 6, 7)
        return half.reshape(sizes[0], model_width // sizes[0] // 2, cols)

    tokens = next_tokens.reshape(-1, sizes[0], 2, model_width // sizes[0] // 2)
    own_tokens = lax.dynamic_index_in_dim(tokens, core, 2, keepdims=False)
    other_tokens = lax.dynamic_index_in_dim(tokens, 1 - core, 2, keepdims=False)
    contract = (((1, 2), (0, 1)), ((), ()))
    summed = lax.dot_general(
        own_tokens, natural(near), contract, preferred_element_type=jnp.float32
    ) + lax.dot_general(
        other_tokens, natural(other), contract, preferred_element_type=jnp.float32
    )
    next_out = summed.astype(jnp.bfloat16)
    return (new_master, new_first, new_second, next_out)


def solution(mesh):
    fine = Mesh(mesh.devices.reshape(4, 2, 4, 2, 4, 2, 2), AXES)
    spec = P(AXES, None)
    return jax.shard_map(
        on_device, mesh=fine, in_specs=(spec,) * 6, out_specs=(spec,) * 4, check_vma=False
    )
```

```python
import functools

import jax
import jax.numpy as jnp
from jax import lax
from jax.experimental import pallas as pl
from jax.experimental.pallas import tpu as pltpu
from jax.sharding import Mesh, PartitionSpec as P

beta_one = 0.9
beta_two = 0.95
learn_rate = 0.003
decay_rate = 0.1
epsilon = 1e-08
steps_done = 10

AXES = ("yf", "ym", "c", "zf", "zm", "zl", "xf", "xm", "xl", "yl")
NEAR = ("zl", "xl", "yl")
MID = ("ym", "zm", "xm")
FAR = ("yf", "zf", "xf")
SWAP = [(0, 1), (1, 0)]
INTERPRET = False


def place(z, x):
    return (z % 2) * 2 + x % 2, (z // 2) * 2 + x // 2


def gradient_body(half_ref, tokens_ref, cotangent_ref, out_ref):
    cot = cotangent_ref[...]
    for z in range(4):
        for zl in range(2):
            at = (z * 2 + zl) * 128
            part = lax.dot_general(
                tokens_ref[:, at : at + 128], cot, (((0,), (0,)), ((), ())),
                preferred_element_type=jnp.float32,
            ).astype(out_ref.dtype)
            for block in range(16):
                x, low = block // 4, block % 4
                mid, far = place(z, x)
                out_ref[zl * 4 + low, 0, mid, 0, far] = part[block * 8 : block * 8 + 8]


def half_gradient(half, tokens_in, cotangent, dtype):
    return pl.pallas_call(
        gradient_body,
        out_shape=jax.ShapeDtypeStruct((8, 2, 4, 2, 4, 8, 128), dtype),
        grid_spec=pltpu.PrefetchScalarGridSpec(
            num_scalar_prefetch=1,
            grid=(4,),
            in_specs=[
                pl.BlockSpec((128, 1024), lambda i, half: (0, i * 2 + half[0])),
                pl.BlockSpec((128, 128), lambda i, half: (0, 0)),
            ],
            out_specs=pl.BlockSpec(
                (8, 1, 4, 1, 4, 8, 128), lambda i, half: (0, i % 2, 0, i // 2, 0, 0, 0)
            ),
        ),
        interpret=INTERPRET,
    )(half, tokens_in, cotangent)


def forward_body(half_ref, tokens_ref, weight_ref, start_ref, out_ref, total_ref):
    step = pl.program_id(0)

    @pl.when(step == 0)
    def _():
        total_ref[...] = start_ref[...]

    total = total_ref[...]
    for z in range(4):
        rows = []
        for zl in range(2):
            for block in range(16):
                x, low = block // 4, block % 4
                mid, far = place(z, x)
                rows.append(weight_ref[zl * 4 + low, 0, mid, 0, far].astype(jnp.float32))
        weight = jnp.concatenate(rows, axis=0).astype(jnp.bfloat16)
        total += jnp.dot(
            tokens_ref[:, z * 256 : z * 256 + 256], weight, preferred_element_type=jnp.float32
        )
    total_ref[...] = total
    out_ref[...] = total.astype(out_ref.dtype)


def half_forward(half, next_tokens, weight, start, dtype):
    rows = next_tokens.shape[0]
    return pl.pallas_call(
        forward_body,
        out_shape=jax.ShapeDtypeStruct((rows, 128), dtype),
        grid_spec=pltpu.PrefetchScalarGridSpec(
            num_scalar_prefetch=1,
            grid=(4,),
            in_specs=[
                pl.BlockSpec((rows, 1024), lambda i, half: (0, i * 2 + half[0])),
                pl.BlockSpec(
                    (8, 1, 4, 1, 4, 8, 128), lambda i, half: (0, i % 2, 0, i // 2, 0, 0, 0)
                ),
                pl.BlockSpec((rows, 128), lambda i, half: (0, 0)),
            ],
            out_specs=pl.BlockSpec((rows, 128), lambda i, half: (0, 0)),
            scratch_shapes=[pltpu.VMEM((rows, 128), jnp.float32)],
        ),
        interpret=INTERPRET,
    )(half, next_tokens, weight, start)


def exchange(value, axes):
    return lax.all_to_all(value, axes, 0, 0, tiled=True)


def summed(value):
    return jnp.sum(value.astype(jnp.float32), axis=0)


def on_device(tokens_in, cotangent, next_tokens, master, first_moment, second_moment):
    core = lax.axis_index("c")
    mine = core.reshape(1).astype(jnp.int32)
    theirs = 1 - mine
    bf16 = jnp.bfloat16

    give = half_gradient(theirs, tokens_in, cotangent, bf16)
    got = lax.ppermute(give, "c", SWAP)
    keep = half_gradient(mine, tokens_in, cotangent, jnp.float32)
    pair = (keep + got.astype(jnp.float32)).astype(bf16)
    near = summed(exchange(pair.reshape(8, 512, 128), NEAR)).astype(bf16)
    mid = summed(exchange(near.reshape(8, 64, 128), MID)).astype(bf16)
    gradient = summed(exchange(mid.reshape(8, 8, 128), FAR))

    new_first = beta_one * first_moment + (1.0 - beta_one) * gradient
    new_second = beta_two * second_moment + (1.0 - beta_two) * gradient * gradient
    first_hat = new_first / (1.0 - beta_one**steps_done)
    second_hat = new_second / (1.0 - beta_two**steps_done)
    new_master = master - learn_rate * (
        first_hat / (jnp.sqrt(second_hat) + epsilon) + decay_rate * master
    )
    low_weight = new_master.astype(bf16)

    far = exchange(jnp.broadcast_to(low_weight, (8, 8, 128)), FAR).reshape(64, 128)
    mid = exchange(jnp.broadcast_to(far, (8, 64, 128)), MID).reshape(512, 128)
    near = exchange(jnp.broadcast_to(mid, (8, 512, 128)), NEAR)
    near = near.reshape(8, 2, 4, 2, 4, 8, 128)
    other = lax.ppermute(near, "c", SWAP)
    rows = next_tokens.shape[0]
    start = jnp.zeros((rows, 128), jnp.float32)
    own_part = half_forward(mine, next_tokens, near, start, jnp.float32)
    next_out = half_forward(theirs, next_tokens, other, own_part, bf16)
    return (new_master, new_first, new_second, next_out)


def solution(mesh):
    fine = Mesh(mesh.devices.reshape(2, 2, 2, 2, 2, 2, 2, 2, 2, 2), AXES)
    spec = P(AXES, None)
    return jax.shard_map(
        on_device, mesh=fine, in_specs=(spec,) * 6, out_specs=(spec,) * 4, check_vma=False
    )
```

```python
import jax
import jax.numpy as jnp
from jax import lax
from jax.experimental import pallas as pl
from jax.experimental.pallas import tpu as pltpu
from jax.sharding import Mesh, PartitionSpec as P

beta_one = 0.9
beta_two = 0.95
learn_rate = 0.003
decay_rate = 0.1
epsilon = 1e-08
steps_done = 10

AXES = ("yh", "c", "zh", "zl", "xh", "xl", "yl")
NEAR = ("zl", "xl", "yl")
FAR = ("yh", "zh", "xh")
SWAP = [(0, 1), (1, 0)]
INTERPRET = False
SMEM = pl.BlockSpec(memory_space=pltpu.SMEM)
VMEM = pl.BlockSpec(memory_space=pltpu.VMEM)


def held(array):
    return array if INTERPRET else pltpu.with_memory_space_constraint(array, pltpu.VMEM)


def in_vmem(shape, dtype):
    return (jax.ShapeDtypeStruct if INTERPRET else pltpu.VMEM)(shape, dtype)


def blocks(half):
    for y in range(4):
        for z in range(4):
            for zl in range(2):
                start = pl.multiple_of(y * 2048 + half * 1024 + (z * 2 + zl) * 128, 128)
                for block in range(16):
                    x, low = block // 4, block % 4
                    yield start + block * 8, (zl * 4 + low, y, z * 4 + x)


def give_body(half_ref, gradient_ref, out_ref):
    for row, place in blocks(half_ref[0]):
        out_ref[place] = gradient_ref[pl.ds(row, 8), :].astype(out_ref.dtype)


def pair_body(half_ref, gradient_ref, got_ref, out_ref):
    for row, place in blocks(half_ref[0]):
        both = gradient_ref[pl.ds(row, 8), :] + got_ref[place].astype(jnp.float32)
        out_ref[place] = both.astype(out_ref.dtype)


def rearranged(body, half, *arrays):
    return pl.pallas_call(
        body,
        out_shape=in_vmem((8, 4, 16, 8, 128), jnp.bfloat16),
        in_specs=[SMEM] + [VMEM] * len(arrays),
        out_specs=VMEM,
        compiler_params=pltpu.CompilerParams(vmem_limit_bytes=16 << 20),
        interpret=INTERPRET,
    )(half, *[held(a) for a in arrays])


def forward_body(half_ref, tokens_ref, weight_ref, start_ref, out_ref):
    total = None if start_ref is None else start_ref[...]
    for y in range(4):
        for z in range(4):
            rows = []
            for zl in range(2):
                for block in range(16):
                    x, low = block // 4, block % 4
                    rows.append(weight_ref[zl * 4 + low, y, z * 4 + x].astype(jnp.float32))
            weight = jnp.concatenate(rows, axis=0).astype(jnp.bfloat16)
            at = pl.multiple_of(y * 2048 + half_ref[0] * 1024 + z * 256, 256)
            part = jnp.dot(
                tokens_ref[:, pl.ds(at, 256)], weight, preferred_element_type=jnp.float32
            )
            total = part if total is None else total + part
    out_ref[...] = total.astype(out_ref.dtype)


def first_body(half_ref, tokens_ref, weight_ref, out_ref):
    forward_body(half_ref, tokens_ref, weight_ref, None, out_ref)


def half_forward(half, next_tokens, weight, start, dtype):
    arrays = (next_tokens, weight) if start is None else (next_tokens, weight, start)
    return pl.pallas_call(
        first_body if start is None else forward_body,
        out_shape=(in_vmem if start is None else jax.ShapeDtypeStruct)(
            (next_tokens.shape[0], 128), dtype
        ),
        in_specs=[SMEM] + [VMEM] * len(arrays),
        out_specs=VMEM,
        compiler_params=pltpu.CompilerParams(vmem_limit_bytes=16 << 20),
        interpret=INTERPRET,
    )(half, *[held(a) for a in arrays])


def exchange(value, axes):
    return lax.all_to_all(value, axes, 0, 0, tiled=True)


def summed(value):
    return jnp.sum(value.astype(jnp.float32), axis=0)


def on_device(tokens_in, cotangent, next_tokens, master, first_moment, second_moment):
    core = lax.axis_index("c")
    mine = core.reshape(1).astype(jnp.int32)
    theirs = 1 - mine
    bf16 = jnp.bfloat16

    local = lax.dot_general(
        tokens_in, cotangent, (((0,), (0,)), ((), ())), preferred_element_type=jnp.float32
    )
    give = rearranged(give_body, theirs, local)
    got = lax.ppermute(give, "c", SWAP)
    pair = rearranged(pair_body, mine, local, got)
    near = summed(exchange(pair.reshape(8, 512, 128), NEAR)).astype(bf16)
    gradient = summed(exchange(near.reshape(64, 8, 128), FAR))

    new_first = beta_one * first_moment + (1.0 - beta_one) * gradient
    new_second = beta_two * second_moment + (1.0 - beta_two) * gradient * gradient
    first_hat = new_first / (1.0 - beta_one**steps_done)
    second_hat = new_second / (1.0 - beta_two**steps_done)
    new_master = master - learn_rate * (
        first_hat / (jnp.sqrt(second_hat) + epsilon) + decay_rate * master
    )
    low_weight = new_master.astype(bf16)

    far = exchange(jnp.broadcast_to(low_weight, (64, 8, 128)), FAR).reshape(512, 128)
    near = exchange(jnp.broadcast_to(far, (8, 512, 128)), NEAR)
    near = near.reshape(8, 4, 16, 8, 128)
    other = lax.ppermute(near, "c", SWAP)
    own_part = half_forward(mine, next_tokens, near, None, jnp.float32)
    next_out = half_forward(theirs, next_tokens, other, own_part, bf16)
    return (new_master, new_first, new_second, next_out)


def solution(mesh):
    fine = Mesh(mesh.devices.reshape(4, 2, 4, 2, 4, 2, 2), AXES)
    spec = P(AXES, None)
    return jax.shard_map(
        on_device, mesh=fine, in_specs=(spec,) * 6, out_specs=(spec,) * 4, check_vma=False
    )
```

```python
import jax
import jax.numpy as jnp
from jax import lax
from jax.experimental import pallas as pl
from jax.experimental.pallas import tpu as pltpu
from jax.sharding import Mesh, PartitionSpec as P

beta_one = 0.9
beta_two = 0.95
learn_rate = 0.003
decay_rate = 0.1
epsilon = 1e-08
steps_done = 10

AXES = ("yh", "c", "zh", "zl", "xh", "xl", "yl")
NEAR = ("zl", "xl", "yl")
FAR = ("yh", "zh", "xh")
SWAP = [(0, 1), (1, 0)]
INTERPRET = False
SMEM = pl.BlockSpec(memory_space=pltpu.SMEM)
VMEM = pl.BlockSpec(memory_space=pltpu.VMEM)


def held(array):
    return array if INTERPRET else pltpu.with_memory_space_constraint(array, pltpu.VMEM)


def in_vmem(shape, dtype):
    return (jax.ShapeDtypeStruct if INTERPRET else pltpu.VMEM)(shape, dtype)


def blocks(half):
    for y in range(4):
        for z in range(4):
            for zl in range(2):
                start = pl.multiple_of(y * 2048 + half * 1024 + (z * 2 + zl) * 128, 128)
                for block in range(16):
                    x, low = block // 4, block % 4
                    yield start + block * 8, (zl * 4 + low, y, z * 4 + x)


def give_body(half_ref, gradient_ref, out_ref):
    for row, place in blocks(half_ref[0]):
        out_ref[place] = gradient_ref[pl.ds(row, 8), :].astype(out_ref.dtype)


def pair_body(half_ref, gradient_ref, got_ref, out_ref):
    for row, place in blocks(half_ref[0]):
        both = gradient_ref[pl.ds(row, 8), :] + got_ref[place].astype(jnp.float32)
        out_ref[place] = both.astype(out_ref.dtype)


def rearranged(body, half, *arrays):
    return pl.pallas_call(
        body,
        out_shape=in_vmem((8, 4, 16, 8, 128), jnp.bfloat16),
        in_specs=[SMEM] + [VMEM] * len(arrays),
        out_specs=VMEM,
        compiler_params=pltpu.CompilerParams(vmem_limit_bytes=16 << 20),
        interpret=INTERPRET,
    )(half, *[held(a) for a in arrays])


def forward_body(half_ref, tokens_ref, weight_ref, out_ref):
    total = jnp.zeros(out_ref.shape, jnp.float32)
    for y in range(4):
        for z in range(4):
            rows = []
            for zl in range(2):
                for block in range(16):
                    x, low = block // 4, block % 4
                    rows.append(weight_ref[zl * 4 + low, y, z * 4 + x].astype(jnp.float32))
            weight = jnp.concatenate(rows, axis=0).astype(jnp.bfloat16)
            at = pl.multiple_of(y * 2048 + half_ref[0] * 1024 + z * 256, 256)
            total += jnp.dot(
                tokens_ref[:, pl.ds(at, 256)], weight, preferred_element_type=jnp.float32
            )
    out_ref[...] = total


def half_forward(half, next_tokens, weight):
    return pl.pallas_call(
        forward_body,
        out_shape=in_vmem((next_tokens.shape[0], 128), jnp.float32),
        in_specs=[SMEM, VMEM, VMEM],
        out_specs=VMEM,
        compiler_params=pltpu.CompilerParams(vmem_limit_bytes=16 << 20),
        interpret=INTERPRET,
    )(half, held(next_tokens), held(weight))


def exchange(value, axes):
    return lax.all_to_all(value, axes, 0, 0, tiled=True)


def summed(value):
    return jnp.sum(value.astype(jnp.float32), axis=0)


def on_device(tokens_in, cotangent, next_tokens, master, first_moment, second_moment):
    core = lax.axis_index("c")
    mine = core.reshape(1).astype(jnp.int32)
    theirs = 1 - mine
    bf16 = jnp.bfloat16

    other_tokens = lax.ppermute(next_tokens, "c", SWAP)
    local = lax.dot_general(
        tokens_in, cotangent, (((0,), (0,)), ((), ())), preferred_element_type=jnp.float32
    )
    give = rearranged(give_body, theirs, local)
    got = lax.ppermute(give, "c", SWAP)
    pair = rearranged(pair_body, mine, local, got)
    near = summed(exchange(pair.reshape(8, 512, 128), NEAR)).astype(bf16)
    near, other_tokens = lax.optimization_barrier((near, other_tokens))
    gradient = summed(exchange(near.reshape(64, 8, 128), FAR))

    new_first = beta_one * first_moment + (1.0 - beta_one) * gradient
    new_second = beta_two * second_moment + (1.0 - beta_two) * gradient * gradient
    first_hat = new_first / (1.0 - beta_one**steps_done)
    second_hat = new_second / (1.0 - beta_two**steps_done)
    new_master = master - learn_rate * (
        first_hat / (jnp.sqrt(second_hat) + epsilon) + decay_rate * master
    )
    low_weight = new_master.astype(bf16)

    far = exchange(jnp.broadcast_to(low_weight, (64, 8, 128)), FAR).reshape(512, 128)
    near = exchange(jnp.broadcast_to(far, (8, 512, 128)), NEAR)
    near = near.reshape(8, 4, 16, 8, 128)
    for_other = half_forward(mine, other_tokens, near)
    from_other = lax.ppermute(for_other, "c", SWAP)
    next_out = (half_forward(mine, next_tokens, near) + from_other).astype(bf16)
    return (new_master, new_first, new_second, next_out)


def solution(mesh):
    fine = Mesh(mesh.devices.reshape(4, 2, 4, 2, 4, 2, 2), AXES)
    spec = P(AXES, None)
    return jax.shard_map(
        on_device, mesh=fine, in_specs=(spec,) * 6, out_specs=(spec,) * 4, check_vma=False
    )
```

```python
import jax
import jax.numpy as jnp
from jax import lax
from jax.experimental import pallas as pl
from jax.experimental.pallas import tpu as pltpu
from jax.sharding import Mesh, PartitionSpec as P

beta_one = 0.9
beta_two = 0.95
learn_rate = 0.003
decay_rate = 0.1
epsilon = 1e-08
steps_done = 10

AXES = ("yh", "c", "zh", "zl", "xh", "xl", "yl")
NEAR = ("zl", "xl", "yl")
FAR = ("yh", "zh", "xh")
SWAP = [(0, 1), (1, 0)]
INTERPRET = False
SMEM = pl.BlockSpec(memory_space=pltpu.SMEM)
VMEM = pl.BlockSpec(memory_space=pltpu.VMEM)


def held(array):
    return array if INTERPRET else pltpu.with_memory_space_constraint(array, pltpu.VMEM)


def in_vmem(shape, dtype):
    return (jax.ShapeDtypeStruct if INTERPRET else pltpu.VMEM)(shape, dtype)


def blocks(half):
    for y in range(4):
        for z in range(4):
            for zl in range(2):
                start = pl.multiple_of(y * 2048 + half * 1024 + (z * 2 + zl) * 128, 128)
                for block in range(16):
                    x, low = block // 4, block % 4
                    yield start + block * 8, (zl * 4 + low, y, z * 4 + x)


def give_body(half_ref, gradient_ref, out_ref):
    for row, place in blocks(half_ref[0]):
        out_ref[place] = gradient_ref[pl.ds(row, 8), :].astype(out_ref.dtype)


def pair_body(half_ref, gradient_ref, got_ref, out_ref):
    for row, place in blocks(half_ref[0]):
        both = gradient_ref[pl.ds(row, 8), :] + got_ref[place].astype(jnp.float32)
        out_ref[place] = both.astype(out_ref.dtype)


def rearranged(body, half, *arrays):
    return pl.pallas_call(
        body,
        out_shape=in_vmem((8, 4, 16, 8, 128), jnp.bfloat16),
        in_specs=[SMEM] + [VMEM] * len(arrays),
        out_specs=VMEM,
        compiler_params=pltpu.CompilerParams(vmem_limit_bytes=16 << 20),
        interpret=INTERPRET,
    )(half, *[held(a) for a in arrays])


def forward_body(half_ref, tokens_ref, weight_ref, out_ref):
    total = jnp.zeros(out_ref.shape, jnp.float32)
    for y in range(4):
        for z in range(4):
            rows = []
            for zl in range(2):
                for block in range(16):
                    x, low = block // 4, block % 4
                    rows.append(weight_ref[zl * 4 + low, y, z * 4 + x].astype(jnp.float32))
            weight = jnp.concatenate(rows, axis=0).astype(jnp.bfloat16)
            at = pl.multiple_of(y * 2048 + half_ref[0] * 1024 + z * 256, 256)
            total += jnp.dot(
                tokens_ref[:, pl.ds(at, 256)], weight, preferred_element_type=jnp.float32
            )
    out_ref[...] = total


def half_forward(half, next_tokens, weight):
    return pl.pallas_call(
        forward_body,
        out_shape=in_vmem((next_tokens.shape[0], 128), jnp.float32),
        in_specs=[SMEM, VMEM, VMEM],
        out_specs=VMEM,
        compiler_params=pltpu.CompilerParams(vmem_limit_bytes=16 << 20),
        interpret=INTERPRET,
    )(half, next_tokens, held(weight))


def exchange(value, axes):
    return lax.all_to_all(value, axes, 0, 0, tiled=True)


def summed(value):
    return jnp.sum(value.astype(jnp.float32), axis=0)


def on_device(tokens_in, cotangent, next_tokens, master, first_moment, second_moment):
    core = lax.axis_index("c")
    mine = core.reshape(1).astype(jnp.int32)
    theirs = 1 - mine
    bf16 = jnp.bfloat16

    other_tokens = lax.ppermute(next_tokens, "c", SWAP)
    local = lax.dot_general(
        tokens_in, cotangent, (((0,), (0,)), ((), ())), preferred_element_type=jnp.float32
    )
    give = rearranged(give_body, theirs, local)
    got = lax.ppermute(give, "c", SWAP)
    got, other_tokens = lax.optimization_barrier((got, other_tokens))
    pair = rearranged(pair_body, mine, local, got)
    near = summed(exchange(pair.reshape(8, 512, 128), NEAR)).astype(bf16)
    gradient = summed(exchange(near.reshape(64, 8, 128), FAR))

    new_first = beta_one * first_moment + (1.0 - beta_one) * gradient
    new_second = beta_two * second_moment + (1.0 - beta_two) * gradient * gradient
    first_hat = new_first / (1.0 - beta_one**steps_done)
    second_hat = new_second / (1.0 - beta_two**steps_done)
    new_master = master - learn_rate * (
        first_hat / (jnp.sqrt(second_hat) + epsilon) + decay_rate * master
    )
    low_weight = new_master.astype(bf16)

    far = exchange(jnp.broadcast_to(low_weight, (64, 8, 128)), FAR).reshape(512, 128)
    near = exchange(jnp.broadcast_to(far, (8, 512, 128)), NEAR)
    near = near.reshape(8, 4, 16, 8, 128)
    for_other = half_forward(mine, other_tokens, near)
    from_other = lax.ppermute(for_other, "c", SWAP)
    next_out = (half_forward(mine, next_tokens, near) + from_other).astype(bf16)
    return (new_master, new_first, new_second, next_out)


def solution(mesh):
    fine = Mesh(mesh.devices.reshape(4, 2, 4, 2, 4, 2, 2), AXES)
    spec = P(AXES, None)
    return jax.shard_map(
        on_device, mesh=fine, in_specs=(spec,) * 6, out_specs=(spec,) * 4, check_vma=False
    )
```
